512 devices in a mesh: section: 8 (over y, core), seq: 64 (over x, z).
Axes of the slice: x: 4, y: 4, z: 16, core: 2. Of those that a mesh axis runs over, the one named last changes fastest.
Arguments:
- slab_rows: bfloat16 [8192, 4096], P('seq'), may hold values from -10 to 10
- filter_taps: bfloat16 [8, 256, 128], P('section', 'seq'), may hold values from -0.5 to 0.5
- skip_weights: bfloat16 [8, 4096], P('section', 'seq'), may hold values from -0.59765625 to 0.59765625
Outputs:
- section_outputs: bfloat16 [8, 8192, 4096], P('section', 'seq')
- tap_hessians: float32 [8, 256, 128, 128], P('section', 'seq')
The draws below stay inside these ranges and needn't reach their ends.
All inputs are finite; a program needn't handle non-finite values.
Results may differ from the reference program's by a relative error of at most 0.0073.
Values may be sent and summed in bfloat16 or wider, within the bound.
No kernel may reach another device: no remote copies, remote signals or barrier semaphores. Data moves between devices by JAX's collectives and lax.ppermute only.
A program may use at most 64 MiB of HBM per device.

```python
import jax
import jax.numpy as jnp
from jax import lax

D = 4096
GROUP = 16
TAPS = 128
LENGTH = 8192
GROUPS = 256
SECTIONS = 8


def draw_slab_rows(key, part):
    drawn = jnp.clip(jax.random.normal(jax.random.fold_in(key, 4), (LENGTH, D), jnp.float32), -6.0, 6.0)
    return drawn.astype(jnp.bfloat16)


def steps_of(rng, dims, split, smallest, high):
    factor_of, own = 1.0, jax.random.fold_in(rng, 6)
    for position, blocks in split:
        steps = jnp.exp(jax.random.uniform(jax.random.fold_in(own, position), (blocks,), jnp.float32, smallest / len(split), high / len(split)))
        factor_of = factor_of * jnp.repeat(steps, dims[position] // blocks).reshape([-1 if axis == position else 1 for axis in range(len(dims))])
    return factor_of


def noise(rng, shape, width, most, pieces=(), kind=jnp.bfloat16):
    loudness = steps_of(rng, shape, pieces, -0.22, 0.18) if pieces else 1.0
    array = jax.random.normal(rng, shape, jnp.float32) * width * loudness
    return jnp.minimum(jnp.maximum(array, -most), most).astype(kind)


def setup_inputs(seed: int = 0) -> dict:
    streams_of = jax.random.split(jax.random.key(seed), 4)
    slab_rows = draw_slab_rows(jax.random.fold_in(streams_of[3], 71), 0)
    filter_taps = noise(streams_of[1], (SECTIONS, GROUPS, TAPS), TAPS ** -0.5, 0.5, ((0, 8), (1, 64)))
    skip_weights = jnp.clip(jax.random.uniform(streams_of[2], (SECTIONS, D), jnp.float32, -0.59765625, 0.59765625) * steps_of(streams_of[2], (SECTIONS, D), ((0, 8), (1, 64)), -0.4, 0.0), -0.59765625, 0.59765625).astype(jnp.bfloat16)
    return dict(slab_rows=slab_rows, filter_taps=filter_taps, skip_weights=skip_weights)


def toeplitz(taps_row):
    out_pos = jnp.arange(TAPS)[:, None]
    in_pos = jnp.arange(2 * TAPS)[None, :]
    lag_index = TAPS + out_pos - in_pos
    active = (lag_index >= 0) & (lag_index < TAPS)
    tap_table = taps_row[:, jnp.clip(lag_index, 0, TAPS - 1)]
    return jnp.where(active[None], tap_table, jnp.zeros_like(tap_table))


def windows(current, earlier):
    nblocks = current.shape[0] // TAPS
    groups_here = current.shape[1] // GROUP
    blocks = current.reshape(nblocks, TAPS, groups_here, GROUP)
    before = jnp.concatenate([earlier.reshape(1, TAPS, groups_here, GROUP), blocks[:-1]], axis=0)
    return jnp.concatenate([before, blocks], axis=1)


def gram_window(window_rows):
    before = window_rows[:, :TAPS]
    present = window_rows[:, TAPS:]
    cur_part = jnp.einsum('nsgc,nrgc->gsr', present, present, preferred_element_type=jnp.float32)
    cross = jnp.einsum('nsgc,nrgc->gsr', before, present, preferred_element_type=jnp.float32)
    first = jnp.einsum('sgc,rgc->gsr', before[0], before[0], preferred_element_type=jnp.float32)
    last = jnp.einsum('sgc,rgc->gsr', present[-1], present[-1], preferred_element_type=jnp.float32)
    prev_part = cur_part - last + first
    top = jnp.concatenate([prev_part, cross], axis=2)
    bottom = jnp.concatenate([jnp.swapaxes(cross, 1, 2), cur_part], axis=2)
    return jnp.concatenate([top, bottom], axis=1)


def diag_prefix(gram_sum):
    running = gram_sum
    size = gram_sum.shape[-1]
    offset = 1
    while offset < size:
        widths = [(0, 0)] * (running.ndim - 2) + [(offset, 0), (offset, 0)]
        running = running + jnp.pad(running, widths)[..., :size, :size]
        offset = offset * 2
    return running


def tap_hessian(gram_sum):
    prefix = diag_prefix(gram_sum)
    return (prefix[..., TAPS:, TAPS:] - prefix[..., :TAPS, :TAPS])[..., ::-1, ::-1]


def reference(slab_rows, filter_taps, skip_weights):
    current = slab_rows
    outputs = []
    hessians = []
    for section_no in range(SECTIONS):
        blocks = windows(current, jnp.zeros((TAPS, D), jnp.bfloat16))
        matrix = toeplitz(filter_taps[section_no]).astype(jnp.float32)
        filtered = jnp.einsum('gts,nsgc->ntgc', matrix, blocks.astype(jnp.float32)).reshape(LENGTH, D)
        filtered = filtered + skip_weights[section_no].astype(jnp.float32)[None, :] * current.astype(jnp.float32)
        grouped = jnp.moveaxis(blocks, 2, 0)
        gram_sum = lax.map(lambda single: gram_window(single.astype(jnp.float32)[:, :, None, :])[0], grouped)
        hessians.append(tap_hessian(gram_sum) * (2.0 / (LENGTH * GROUP)))
        current = filtered.astype(jnp.bfloat16)
        outputs.append(current)
    return jnp.stack(outputs), jnp.stack(hessians)
```

```python
import functools

import jax
import jax.numpy as jnp
from jax import lax
from jax.experimental import pallas as pl
from jax.experimental.pallas import tpu as pltpu
from jax.sharding import PartitionSpec as P

GROUP = 16
TAPS = 128
HALF = 8
EDGE = 2 * HALF
INFO = 2 * EDGE
CHUNK = 1024

VMEM = pltpu.VMEM
SMEM = pltpu.SMEM


def pick_kernel(sec_ref, slab_ref, out_ref):
    sec = sec_ref[0]
    width = 256
    rows = width // 8
    out_row = lax.broadcasted_iota(jnp.int32, (rows, width), 0)
    lane = lax.broadcasted_iota(jnp.int32, (rows, width), 1)
    wanted = (out_row // HALF) * 64 + sec * HALF + out_row % HALF
    chosen = jnp.where(lane == wanted, 1.0, 0.0).astype(jnp.bfloat16)
    for piece in range(CHUNK // width):
        part = lax.dot_general(
            chosen,
            slab_ref[:, piece * width : (piece + 1) * width],
            (((1,), (1,)), ((), ())),
            preferred_element_type=jnp.float32,
        )
        out_ref[piece * rows : (piece + 1) * rows, :] = part.astype(jnp.bfloat16)


def pick(sec, slab_rows):
    length, width = slab_rows.shape
    return pl.pallas_call(
        pick_kernel,
        grid_spec=pltpu.PrefetchScalarGridSpec(
            num_scalar_prefetch=1,
            grid=(width // CHUNK,),
            in_specs=[pl.BlockSpec((length, CHUNK), lambda i, s: (0, i))],
            out_specs=pl.BlockSpec((CHUNK // 8, length), lambda i, s: (i, 0)),
        ),
        out_shape=jax.ShapeDtypeStruct((width // 8, length), jnp.bfloat16),
        name="pick",
    )(sec, slab_rows)


def chain_kernel(sec_ref, x_ref, par_ref, y_ref, info_ref, state, par):
    step = pl.program_id(0)
    sec = sec_ref[0]
    rows = state.shape[0]

    @pl.when(step == 0)
    def _():
        state[...] = x_ref[...].astype(jnp.float32)
        par[...] = par_ref[...].astype(jnp.float32)

    slot = step ^ sec
    taps_row = par[pl.ds(slot * 8 + sec // 2, 1), :]
    skip_row = par[pl.ds(slot * 8 + 4, 1), :]
    spread = jnp.concatenate([taps_row, jnp.zeros_like(taps_row)], axis=1)
    spread = jnp.broadcast_to(spread, (TAPS, 2 * TAPS))
    band = pltpu.roll(spread, 0, 1, stride=1, stride_axis=0).astype(jnp.bfloat16)
    lane = lax.broadcasted_iota(jnp.int32, (HALF, TAPS), 1)
    chan = lax.broadcasted_iota(jnp.int32, (HALF, TAPS), 0)
    own = jnp.where(lane == sec * HALF + chan, jnp.broadcast_to(skip_row, (HALF, TAPS)), 0.0)
    gain = jnp.broadcast_to(jnp.sum(own, axis=1, keepdims=True), (HALF, TAPS))

    current = state[...]
    current_b = current.astype(jnp.bfloat16)
    both = jnp.dot(current_b, band, preferred_element_type=jnp.float32)
    blank = jnp.zeros((HALF, TAPS), jnp.float32)
    carried = jnp.concatenate([blank, both[: rows - HALF, TAPS:]], axis=0)
    direct = (current.reshape(rows // HALF, HALF, TAPS) * gain[None]).reshape(rows, TAPS)
    filtered = (both[:, :TAPS] + carried + direct).astype(jnp.bfloat16)
    y_ref[0] = filtered
    state[...] = filtered.astype(jnp.float32)

    body = jnp.concatenate([current[: rows - HALF], blank], axis=0)
    after = jnp.concatenate([body[HALF:], blank], axis=0)
    pair = jnp.concatenate([body, after], axis=1).astype(jnp.bfloat16)
    gram = lax.dot_general(
        current_b, pair, (((0,), (0,)), ((), ())), preferred_element_type=jnp.float32
    )
    size = TAPS
    while size > 8:
        size = size // 2
        gram = gram[:size] + pltpu.roll(gram[size:], 2 * TAPS - size, 1)
    row = lax.broadcasted_iota(jnp.int32, gram.shape, 0)
    for bit in (4, 2, 1):
        gram = jnp.where((row & bit) != 0, pltpu.roll(gram, 2 * TAPS - bit, 1), gram)
    lags = jnp.sum(gram, axis=0, keepdims=True)[:, :TAPS]
    high = lags.astype(jnp.bfloat16).astype(jnp.float32)
    middle = (lags - high).astype(jnp.bfloat16).astype(jnp.float32)
    low = lags - high - middle
    info_row = lax.broadcasted_iota(jnp.int32, (INFO - EDGE, TAPS), 0)
    packed = jnp.where(
        info_row == 0, high, jnp.where(info_row == 1, middle, jnp.where(info_row == 2, low, 0.0))
    )
    info = jnp.concatenate([current[rows - EDGE :], packed], axis=0)
    info_ref[slot] = info.astype(jnp.bfloat16)


def chain(sec, rows_in, params, sections):
    rows = rows_in.shape[0]
    return pl.pallas_call(
        chain_kernel,
        grid_spec=pltpu.PrefetchScalarGridSpec(
            num_scalar_prefetch=1,
            grid=(sections,),
            in_specs=[
                pl.BlockSpec((rows, TAPS), lambda i, s: (0, 0)),
                pl.BlockSpec(params.shape, lambda i, s: (0, 0)),
            ],
            out_specs=[
                pl.BlockSpec((1, rows, TAPS), lambda i, s: (i, 0, 0)),
                pl.BlockSpec((sections, INFO, TAPS), lambda i, s: (0, 0, 0)),
            ],
            scratch_shapes=[VMEM((rows, TAPS), jnp.float32), VMEM(params.shape, jnp.float32)],
        ),
        out_shape=[
            jax.ShapeDtypeStruct((sections, rows, TAPS), jnp.bfloat16),
            jax.ShapeDtypeStruct((sections, INFO, TAPS), jnp.bfloat16),
        ],
        name="chain",
    )(sec, rows_in, params)


def place_kernel(x_ref, out_ref):
    quads = x_ref.shape[1]
    row = lax.broadcasted_iota(jnp.int32, (TAPS, TAPS), 0)
    col = lax.broadcasted_iota(jnp.int32, (TAPS, TAPS), 1)
    same = jnp.where(row == col, 1.0, 0.0).astype(jnp.bfloat16)
    for pair in range(quads // 2):
        parts = [x_ref[r, 2 * pair + half] for half in range(2) for r in range(8)]
        tile = jnp.concatenate(parts, axis=0)
        turned = lax.dot_general(
            same, tile, (((1,), (1,)), ((), ())), preferred_element_type=jnp.float32
        )
        out_ref[:, pair * TAPS : (pair + 1) * TAPS] = turned.astype(jnp.bfloat16)


def place(pieces):
    sections, count, half, length = pieces.shape
    step = 16
    return pl.pallas_call(
        place_kernel,
        grid=(count // step,),
        in_specs=[pl.BlockSpec((sections, step, half, length), lambda i: (0, i, 0, 0))],
        out_specs=pl.BlockSpec((length, step * sections * half), lambda i: (0, i)),
        out_shape=jax.ShapeDtypeStruct((length, count * sections * half), jnp.bfloat16),
        name="place",
    )(pieces)


def swap_bit(value, bit, count):
    return lax.ppermute(value, "section", [(i, i ^ bit) for i in range(count)])


def per_device(slab_rows, filter_taps, skip_weights):
    sections = lax.axis_size("section")
    seq = lax.axis_size("seq")
    section = lax.axis_index("section")
    sec = section.astype(jnp.int32).reshape(1)

    own_params = jnp.concatenate(
        [filter_taps[0], jnp.pad(skip_weights, ((0, 3), (0, TAPS - skip_weights.shape[1])))], axis=0
    )
    params = own_params[None]
    for bit in (1, 2, 4):
        params = jnp.concatenate([params, swap_bit(params, bit, sections)], axis=0)
    params = params.reshape(sections * 8, TAPS)

    picked = pick(sec, slab_rows)
    moved = lax.all_to_all(
        picked.reshape(seq, HALF, TAPS), "seq", split_axis=0, concat_axis=0, tiled=True
    )
    outputs, info = chain(sec, moved.reshape(seq * HALF, TAPS), params, sections)
    pieces = lax.all_to_all(
        outputs.reshape(sections * seq, HALF, TAPS),
        ("section", "seq"),
        split_axis=0,
        concat_axis=0,
        tiled=True,
    )

    info = info.reshape(2, 2, 2, INFO, TAPS)
    for axis, bit in ((2, 1), (1, 2), (0, 4)):
        keep, send = jnp.split(info, 2, axis=axis)
        info = jnp.concatenate([keep, swap_bit(send, bit, sections)], axis=axis)
    for axis, bit in ((2, 1), (1, 2), (0, 4)):
        info = jnp.where((section & bit) != 0, jnp.flip(info, axis), info)
    info = info.reshape(sections // 2, 2, INFO, TAPS)
    groups_here = sections // 2
    before = info[:, :, :HALF, ::-1].reshape(groups_here, GROUP, TAPS)
    last = info[:, :, HALF:EDGE, ::-1].reshape(groups_here, GROUP, TAPS)
    lags = jnp.sum(info[:, :, EDGE : EDGE + 3].astype(jnp.float32), axis=(1, 2))
    running = jnp.einsum(
        "gci,gcl->gil", last, jnp.concatenate([last, before], axis=2),
        preferred_element_type=jnp.float32,
    )
    is_last = (jnp.arange(TAPS) == TAPS - 1)[None, :, None]
    running = running + jnp.where(is_last, jnp.pad(lags, ((0, 0), (TAPS - 1, 1)))[:, None], 0.0)
    offset = 1
    while offset < TAPS:
        running = running + jnp.pad(
            running[:, offset:, offset:], ((0, 0), (0, offset), (0, offset))
        )
        offset = offset * 2
    upper = running[:, :, :TAPS]
    ahead = jnp.arange(TAPS)[None, :] >= jnp.arange(TAPS)[:, None]
    hessians = jnp.where(ahead[None], upper, jnp.swapaxes(upper, 1, 2))
    hessians = hessians * (2.0 / (seq * TAPS * GROUP))

    restored = place(pieces.reshape(sections, seq, HALF, TAPS))
    return (restored[None], hessians[None])


def solution(mesh):
    in_specs = (P("seq", None), P("section", "seq", None), P("section", "seq"))
    out_specs = (P("section", "seq", None), P("section", "seq", None, None))
    return jax.shard_map(
        per_device, mesh=mesh, in_specs=in_specs, out_specs=out_specs, check_vma=False
    )
```

```python
import jax
import jax.numpy as jnp
from jax import lax
from jax.experimental import pallas as pl
from jax.experimental.pallas import tpu as pltpu
from jax.sharding import PartitionSpec as P

GROUP = 16
TAPS = 128
HALF = 8
EDGE = 2 * HALF
INFO = 2 * EDGE
PARTS = 4
CHUNK = 1024
VMEM_LIMIT = 16 * 1024 * 1024


def limits():
    return pltpu.CompilerParams(vmem_limit_bytes=VMEM_LIMIT)


def pick_kernel(sec_ref, slab_ref, out_ref):
    sec = sec_ref[0]
    width = 256
    rows = width // 8
    out_row = lax.broadcasted_iota(jnp.int32, (rows, width), 0)
    lane = lax.broadcasted_iota(jnp.int32, (rows, width), 1)
    wanted = (out_row // HALF) * 64 + sec * HALF + out_row % HALF
    chosen = jnp.where(lane == wanted, 1.0, 0.0).astype(jnp.bfloat16)
    for piece in range(slab_ref.shape[1] // width):
        turned = lax.dot_general(
            chosen,
            slab_ref[:, piece * width : (piece + 1) * width],
            (((1,), (1,)), ((), ())),
            preferred_element_type=jnp.float32,
        )
        out_ref[piece * rows : (piece + 1) * rows, :] = turned.astype(jnp.bfloat16)


def pick(sec, slab_rows):
    length, width = slab_rows.shape
    return pl.pallas_call(
        pick_kernel,
        in_specs=[pl.BlockSpec(memory_space=pltpu.SMEM), pl.BlockSpec(memory_space=pltpu.VMEM)],
        out_specs=pl.BlockSpec(memory_space=pltpu.VMEM),
        out_shape=jax.ShapeDtypeStruct((width // 8, length), jnp.bfloat16),
        compiler_params=limits(),
        name="pick",
    )(sec, slab_rows)


def chain_kernel(sec_ref, x_ref, par_ref, out_ref, par, y_ref, sems):
    sec = sec_ref[0]
    sections, rows, _ = y_ref.shape
    par[...] = par_ref[...].astype(jnp.float32)
    lane = lax.broadcasted_iota(jnp.int32, (HALF, TAPS), 1)
    chan = lax.broadcasted_iota(jnp.int32, (HALF, TAPS), 0)
    blank = jnp.zeros((HALF, TAPS), jnp.float32)
    current_b = x_ref[...]
    copies = []
    for step in range(sections):
        slot = sec ^ step
        taps_row = par[pl.ds(slot * 8 + sec // 2, 1), :]
        skip_row = par[pl.ds(slot * 8 + 4, 1), :]
        spread = jnp.concatenate([taps_row, jnp.zeros_like(taps_row)], axis=1)
        spread = jnp.broadcast_to(spread, (TAPS, 2 * TAPS))
        band = pltpu.roll(spread, 0, 1, stride=1, stride_axis=0).astype(jnp.bfloat16)
        own = jnp.where(lane == sec * HALF + chan, jnp.broadcast_to(skip_row, (HALF, TAPS)), 0.0)
        gain = jnp.broadcast_to(jnp.sum(own, axis=1, keepdims=True), (HALF, TAPS))
        both = jnp.dot(current_b, band, preferred_element_type=jnp.float32)
        carried = jnp.concatenate([blank, both[: rows - HALF, TAPS:]], axis=0)
        current = current_b.astype(jnp.float32)
        direct = (current.reshape(rows // HALF, HALF, TAPS) * gain[None]).reshape(rows, TAPS)
        current_b = (both[:, :TAPS] + carried + direct).astype(jnp.bfloat16)
        y_ref[step] = current_b
        copies.append(pltpu.make_async_copy(y_ref.at[step], out_ref.at[step], sems.at[step]))
        copies[-1].start()
    for copy in copies:
        copy.wait()


def chain(sec, rows_in, params, sections):
    rows = rows_in.shape[0]
    return pl.pallas_call(
        chain_kernel,
        in_specs=[pl.BlockSpec(memory_space=pltpu.SMEM)] + [pl.BlockSpec(memory_space=pltpu.VMEM)] * 2,
        out_specs=pl.BlockSpec(memory_space=pl.ANY),
        out_shape=jax.ShapeDtypeStruct((sections, rows, TAPS), jnp.bfloat16),
        scratch_shapes=[
            pltpu.VMEM(params.shape, jnp.float32),
            pltpu.VMEM((sections, rows, TAPS), jnp.bfloat16),
            pltpu.SemaphoreType.DMA((sections,)),
        ],
        compiler_params=limits(),
        name="chain",
    )(sec, rows_in, params)


def lags_kernel(sec_ref, x_ref, y_ref, info_ref):
    sec = sec_ref[0]
    sections, rows, _ = y_ref.shape
    blank = jnp.zeros((HALF, TAPS), jnp.float32)

    def one(step, source):
        current_b = source
        current = current_b.astype(jnp.float32)
        body = jnp.concatenate([current[: rows - HALF], blank], axis=0)
        after = jnp.concatenate([body[HALF:], blank], axis=0)
        pair = jnp.concatenate([body, after], axis=1).astype(jnp.bfloat16)
        gram = lax.dot_general(
            current_b, pair, (((0,), (0,)), ((), ())), preferred_element_type=jnp.float32
        )
        size = TAPS
        while size > 8:
            size = size // 2
            gram = gram[:size] + pltpu.roll(gram[size:], 2 * TAPS - size, 1)
        row = lax.broadcasted_iota(jnp.int32, gram.shape, 0)
        for bit in (4, 2, 1):
            gram = jnp.where((row & bit) != 0, pltpu.roll(gram, 2 * TAPS - bit, 1), gram)
        lags = jnp.sum(gram, axis=0, keepdims=True)[:, :TAPS]
        high = lags.astype(jnp.bfloat16).astype(jnp.float32)
        middle = (lags - high).astype(jnp.bfloat16).astype(jnp.float32)
        low = lags - high - middle
        info_row = lax.broadcasted_iota(jnp.int32, (INFO - EDGE, TAPS), 0)
        packed = jnp.where(
            info_row == 0,
            high,
            jnp.where(info_row == 1, middle, jnp.where(info_row == 2, low, 0.0)),
        )
        info = jnp.concatenate([current[rows - EDGE :], packed], axis=0)
        info_ref[step ^ sec] = info.astype(jnp.bfloat16)

    one(0, x_ref[...])

    @pl.loop(1, sections)
    def _(step):
        one(step, y_ref[step - 1])


def lag_info(sec, rows_in, outputs):
    sections, rows, _ = outputs.shape
    return pl.pallas_call(
        lags_kernel,
        in_specs=[pl.BlockSpec(memory_space=pltpu.SMEM)] + [pl.BlockSpec(memory_space=pltpu.VMEM)] * 2,
        out_specs=pl.BlockSpec(memory_space=pltpu.VMEM),
        out_shape=jax.ShapeDtypeStruct((sections, INFO, TAPS), jnp.bfloat16),
        compiler_params=limits(),
        cost_estimate=pl.CostEstimate(
            flops=sections * 4 * rows * TAPS * TAPS, bytes_accessed=2 * outputs.size, transcendentals=0
        ),
        name="lags",
    )(sec, rows_in, outputs)


def place_kernel(x_ref, out_ref, turned, sems):
    quads = x_ref.shape[1]
    share = quads // PARTS
    copies = []
    for part in range(PARTS):
        for pair in range(part * share // 2, (part + 1) * share // 2):
            parts = [x_ref[r, 2 * pair + half] for half in range(2) for r in range(8)]
            tile = jnp.concatenate(parts, axis=0)
            turned[:, pair * TAPS : (pair + 1) * TAPS] = tile.T
        span = pl.ds(part * CHUNK, CHUNK)
        copies.append(pltpu.make_async_copy(turned.at[:, span], out_ref.at[:, span], sems.at[part]))
        copies[-1].start()
    for copy in copies:
        copy.wait()


def place(pieces):
    sections, count, half, length = pieces.shape
    width = count * sections * half
    return pl.pallas_call(
        place_kernel,
        in_specs=[pl.BlockSpec(memory_space=pltpu.VMEM)],
        out_specs=pl.BlockSpec(memory_space=pl.ANY),
        out_shape=jax.ShapeDtypeStruct((length, width), jnp.bfloat16),
        scratch_shapes=[pltpu.VMEM((length, width), jnp.bfloat16), pltpu.SemaphoreType.DMA((PARTS,))],
        compiler_params=limits(),
        name="place",
    )(pieces)


def swap_bit(value, bit, count):
    return lax.ppermute(value, "section", [(i, i ^ bit) for i in range(count)])


def per_device(slab_rows, filter_taps, skip_weights):
    sections = lax.axis_size("section")
    seq = lax.axis_size("seq")
    section = lax.axis_index("section")
    sec = section.astype(jnp.int32).reshape(1)

    own_params = jnp.concatenate(
        [filter_taps[0], jnp.pad(skip_weights, ((0, 3), (0, TAPS - skip_weights.shape[1])))], axis=0
    )
    params = own_params[None]
    params = jnp.concatenate([params, swap_bit(params, 1, sections)], axis=0)
    params = jnp.concatenate([params] + [swap_bit(params, bits, sections) for bits in (2, 4, 6)], axis=0)
    params = params.reshape(sections * 8, TAPS)

    picked = pick(sec, slab_rows)
    moved = lax.all_to_all(
        picked.reshape(seq, HALF, TAPS), "seq", split_axis=0, concat_axis=0, tiled=True
    )
    rows_in = moved.reshape(seq * HALF, TAPS)
    outputs = chain(sec, rows_in, params, sections)
    pieces = lax.all_to_all(
        outputs.reshape(sections * seq, HALF, TAPS),
        ("section", "seq"),
        split_axis=0,
        concat_axis=0,
        tiled=True,
    )

    info = lag_info(sec, rows_in, outputs).reshape(2, 2, 2, INFO, TAPS)
    for axis, bit in ((2, 1), (1, 2), (0, 4)):
        keep, send = jnp.split(info, 2, axis=axis)
        info = jnp.concatenate([keep, swap_bit(send, bit, sections)], axis=axis)
    for axis, bit in ((2, 1), (1, 2), (0, 4)):
        info = jnp.where((section & bit) != 0, jnp.flip(info, axis), info)
    info = info.reshape(sections // 2, 2, INFO, TAPS)
    groups_here = sections // 2
    before = info[:, :, :HALF, ::-1].reshape(groups_here, GROUP, TAPS)
    last = info[:, :, HALF:EDGE, ::-1].reshape(groups_here, GROUP, TAPS)
    lags = jnp.sum(info[:, :, EDGE : EDGE + 3].astype(jnp.float32), axis=(1, 2))
    running = jnp.einsum(
        "gci,gcl->gil", last, jnp.concatenate([last, before], axis=2),
        preferred_element_type=jnp.float32,
    )
    is_last = (jnp.arange(TAPS) == TAPS - 1)[None, :, None]
    running = running + jnp.where(is_last, jnp.pad(lags, ((0, 0), (TAPS - 1, 1)))[:, None], 0.0)
    offset = 1
    while offset < TAPS:
        running = running + jnp.pad(
            running[:, offset:, offset:], ((0, 0), (0, offset), (0, offset))
        )
        offset = offset * 2
    upper = running[:, :, :TAPS]
    ahead = jnp.arange(TAPS)[None, :] >= jnp.arange(TAPS)[:, None]
    hessians = jnp.where(ahead[None], upper, jnp.swapaxes(upper, 1, 2))
    hessians = hessians * (2.0 / (seq * TAPS * GROUP))

    restored = place(pieces.reshape(sections, seq, HALF, TAPS))
    return (restored[None], hessians[None])


def solution(mesh):
    in_specs = (P("seq", None), P("section", "seq", None), P("section", "seq"))
    out_specs = (P("section", "seq", None), P("section", "seq", None, None))
    return jax.shard_map(
        per_device, mesh=mesh, in_specs=in_specs, out_specs=out_specs, check_vma=False
    )
```

```python
import jax
import jax.numpy as jnp
from jax import lax
from jax.experimental import pallas as pl
from jax.experimental.pallas import tpu as pltpu
from jax.sharding import Mesh, PartitionSpec as P

GROUP = 16
TAPS = 128
QUARTERS = 4
WIDE = 32
SPAN = 256
EDGE = 2 * GROUP
INFO = EDGE + 16
MIB = 1024 * 1024
EVERY = ("section", "x", "quarter", "slot")


def limits(mib):
    return pltpu.CompilerParams(vmem_limit_bytes=mib * MIB)


def pick_kernel(sec_ref, slab_ref, out_ref, held, sems):
    sec = sec_ref[0]
    copies = []
    for x in range(4):
        start = pl.multiple_of(x * 1024 + (sec // 2) * SPAN, SPAN)
        copies.append(pltpu.make_async_copy(slab_ref.at[:, pl.ds(start, SPAN)], held.at[x], sems.at[x]))
        copies[-1].start()
    rows = SPAN // 2
    out_row = lax.broadcasted_iota(jnp.int32, (rows, SPAN), 0)
    lane = lax.broadcasted_iota(jnp.int32, (rows, SPAN), 1)
    wanted = (out_row // WIDE) * 64 + (sec % 2) * WIDE + out_row % WIDE
    chosen = jnp.where(lane == wanted, 1.0, 0.0).astype(jnp.bfloat16)
    for x in range(4):
        copies[x].wait()
        turned = lax.dot_general(
            chosen, held[x], (((1,), (1,)), ((), ())), preferred_element_type=jnp.float32
        ).astype(jnp.bfloat16)
        for quarter in range(QUARTERS):
            out_ref[x * QUARTERS + quarter] = turned


def pick(sec, slab_rows):
    length = slab_rows.shape[0]
    return pl.pallas_call(
        pick_kernel,
        in_specs=[pl.BlockSpec(memory_space=pltpu.SMEM), pl.BlockSpec(memory_space=pl.ANY)],
        out_specs=pl.BlockSpec(memory_space=pltpu.VMEM),
        out_shape=jax.ShapeDtypeStruct((4 * QUARTERS, SPAN // 2, length), jnp.bfloat16),
        scratch_shapes=[pltpu.VMEM((4, length, SPAN), jnp.bfloat16), pltpu.SemaphoreType.DMA((4,))],
        name="pick",
    )(sec, slab_rows)


def chain_kernel(where_ref, x_ref, par_ref, out_ref, kept_ref, par, y_ref, sems, kept_sems):
    sec = where_ref[0]
    quarter = where_ref[1]
    sections = out_ref.shape[0]
    blocks = x_ref.shape[0]
    share = 16
    par[...] = par_ref[...].astype(jnp.float32)
    lane = lax.broadcasted_iota(jnp.int32, (GROUP, TAPS), 1)
    chan = lax.broadcasted_iota(jnp.int32, (GROUP, TAPS), 0)
    copies = []
    for step in range(sections):
        slot = (step // 2) ^ quarter
        slot = 2 * slot + ((step % 2) ^ (sec % 2))

        def source(first, last, low):
            if step == 0:
                return x_ref[first:last, low : low + GROUP, :]
            return y_ref[step - 1, first:last, low : low + GROUP, :]

        skip_row = jnp.broadcast_to(par[pl.ds(slot * 8 + 4, 1), :], (GROUP, TAPS))
        for part in range(WIDE // GROUP):
            low = part * GROUP
            taps_row = par[pl.ds(slot * 8 + 2 * (sec % 2) + part, 1), :]
            spread = jnp.concatenate([taps_row, jnp.zeros_like(taps_row)], axis=1)
            spread = jnp.broadcast_to(spread, (TAPS, 2 * TAPS))
            band = pltpu.roll(spread, 0, 1, stride=1, stride_axis=0).astype(jnp.bfloat16)
            own = jnp.where(lane == (sec % 2) * WIDE + low + chan, skip_row, 0.0)
            gain = jnp.broadcast_to(jnp.sum(own, axis=1, keepdims=True), (GROUP, TAPS))
            carry = jnp.zeros((GROUP, TAPS), jnp.float32)
            for first in range(0, blocks, share):
                current = source(first, first + share, low).reshape(share * GROUP, TAPS)
                both = jnp.dot(current, band, preferred_element_type=jnp.float32)
                carried = jnp.concatenate([carry, both[: (share - 1) * GROUP, TAPS:]], axis=0)
                carry = both[(share - 1) * GROUP :, TAPS:]
                direct = current.astype(jnp.float32).reshape(share, GROUP, TAPS) * gain[None]
                filtered = both[:, :TAPS] + carried + direct.reshape(share * GROUP, TAPS)
                y_ref[step, first : first + share, low : low + GROUP, :] = filtered.astype(
                    jnp.bfloat16
                ).reshape(share, GROUP, TAPS)
        for x in range(4):
            begin = 16 * x + 4 * quarter
            copies.append(
                pltpu.make_async_copy(
                    y_ref.at[step, pl.ds(begin, 4)], out_ref.at[step, x], sems.at[step, x]
                )
            )
            copies[-1].start()
        if step + 1 < sections:
            copies.append(
                pltpu.make_async_copy(y_ref.at[step], kept_ref.at[step], kept_sems.at[step])
            )
            copies[-1].start()
    for copy in copies:
        copy.wait()


def chain(where, rows_in, params, sections):
    blocks = rows_in.shape[0]
    return pl.pallas_call(
        chain_kernel,
        in_specs=[pl.BlockSpec(memory_space=pltpu.SMEM)] + [pl.BlockSpec(memory_space=pltpu.VMEM)] * 2,
        out_specs=[pl.BlockSpec(memory_space=pl.ANY)] * 2,
        out_shape=[
            jax.ShapeDtypeStruct((sections, 4, 4, WIDE, TAPS), jnp.bfloat16),
            pltpu.HBM((sections - 1, blocks, WIDE, TAPS), jnp.bfloat16),
        ],
        scratch_shapes=[
            pltpu.VMEM(params.shape, jnp.float32),
            pltpu.VMEM((sections, blocks, WIDE, TAPS), jnp.bfloat16),
            pltpu.SemaphoreType.DMA((sections, 4)),
            pltpu.SemaphoreType.DMA((sections - 1,)),
        ],
        compiler_params=limits(24),
        name="chain",
    )(where, rows_in, params)


def lags_kernel(where_ref, x_ref, y_ref, info_ref):
    quarter = where_ref[1]
    sections, blocks = y_ref.shape[0] + 1, y_ref.shape[1]
    rows = (blocks - 1) * GROUP
    blank = jnp.zeros((GROUP, TAPS), jnp.bfloat16)
    for step in range(sections):
        slot = (step // 2) ^ quarter
        for part in range(WIDE // GROUP):
            low = part * GROUP
            if step == 0:
                whole = x_ref[:, low : low + GROUP, :]
            else:
                whole = y_ref[step - 1, :, low : low + GROUP, :]
            body = whole[: blocks - 1].reshape(rows, TAPS)
            after = jnp.concatenate([body[GROUP:], blank], axis=0)
            pair = jnp.concatenate([body, after], axis=1)
            gram = lax.dot_general(
                body, pair, (((0,), (0,)), ((), ())), preferred_element_type=jnp.float32
            )
            size = TAPS
            while size > 8:
                size = size // 2
                gram = gram[:size] + pltpu.roll(gram[size:], 2 * TAPS - size, 1)
            row = lax.broadcasted_iota(jnp.int32, gram.shape, 0)
            for bit in (4, 2, 1):
                gram = jnp.where((row & bit) != 0, pltpu.roll(gram, 2 * TAPS - bit, 1), gram)
            lags = jnp.sum(gram, axis=0, keepdims=True)[:, :TAPS]
            high = lags.astype(jnp.bfloat16).astype(jnp.float32)
            middle = (lags - high).astype(jnp.bfloat16).astype(jnp.float32)
            rest = lags - high - middle
            info_row = lax.broadcasted_iota(jnp.int32, (INFO - EDGE, TAPS), 0)
            packed = jnp.where(
                info_row == 0,
                high,
                jnp.where(info_row == 1, middle, jnp.where(info_row == 2, rest, 0.0)),
            )
            edge = whole[blocks - 2 :].reshape(EDGE, TAPS)
            piece = jnp.concatenate([edge, packed.astype(jnp.bfloat16)], axis=0)
            info_ref[slot, step % 2, part] = piece


def lag_info(where, rows_in, states):
    sections = states.shape[0] + 1
    return pl.pallas_call(
        lags_kernel,
        in_specs=[pl.BlockSpec(memory_space=pltpu.SMEM)] + [pl.BlockSpec(memory_space=pltpu.VMEM)] * 2,
        out_specs=pl.BlockSpec(memory_space=pltpu.VMEM),
        out_shape=jax.ShapeDtypeStruct((sections // 2, 2, WIDE // GROUP, INFO, TAPS), jnp.bfloat16),
        compiler_params=limits(16),
        cost_estimate=pl.CostEstimate(
            flops=4 * states.size * TAPS, bytes_accessed=2 * states.size, transcendentals=0
        ),
        name="lags",
    )(where, rows_in, states)


def place_kernel(x_ref, out_ref, turned, sems):
    copies = []
    for x in range(4):
        for fourth in range(4):
            for pair in range(2):
                parts = [
                    x_ref[2 * fourth + half, x, 2 * pair + slot]
                    for slot in range(2)
                    for half in range(2)
                ]
                tile = jnp.concatenate(parts, axis=0)
                at = 1024 * x + SPAN * fourth + TAPS * pair
                turned[:, at : at + TAPS] = tile.T
        span = pl.ds(x * 1024, 1024)
        copies.append(pltpu.make_async_copy(turned.at[:, span], out_ref.at[:, span], sems.at[x]))
        copies[-1].start()
    for copy in copies:
        copy.wait()


def place(pieces):
    width = pieces.size // TAPS
    return pl.pallas_call(
        place_kernel,
        in_specs=[pl.BlockSpec(memory_space=pltpu.VMEM)],
        out_specs=pl.BlockSpec(memory_space=pl.ANY),
        out_shape=jax.ShapeDtypeStruct((TAPS, width), jnp.bfloat16),
        scratch_shapes=[pltpu.VMEM((TAPS, width), jnp.bfloat16), pltpu.SemaphoreType.DMA((4,))],
        compiler_params=limits(16),
        name="place",
    )(pieces)


def device(section, x, quarter, slot):
    return ((section * 4 + x) * QUARTERS + quarter) * 4 + slot


def turn_params(value):
    pairs = []
    for x in range(4):
        for slot in range(4):
            for quarter in range(QUARTERS):
                for chip in range(4):
                    for core in range(2):
                        origin = device(2 * chip + core, x, quarter, slot)
                        pairs.append((origin, device(2 * quarter + core, x, chip, slot)))
    return lax.ppermute(value, EVERY, pairs)


def home_round(value, offset):
    pairs = []
    for x in range(4):
        for slot in range(4):
            for quarter in range(QUARTERS):
                for core in range(2):
                    origin = device(2 * quarter + core, x, quarter, slot)
                    pairs.append((origin, device(2 * (quarter ^ offset) + core, x, quarter, slot)))
    return lax.ppermute(value, EVERY, pairs)


def swap_cores(value):
    return lax.ppermute(value, "section", [(i, i ^ 1) for i in range(8)])


def per_device(slab_rows, filter_taps, skip_weights):
    sections = lax.axis_size("section")
    section = lax.axis_index("section").astype(jnp.int32)
    quarter = lax.axis_index("quarter").astype(jnp.int32)
    sec = section.reshape(1)
    where = jnp.stack([section, quarter])

    own_params = jnp.concatenate(
        [filter_taps[0], jnp.pad(skip_weights, ((0, 3), (0, TAPS - skip_weights.shape[1])))], axis=0
    )[None]
    params = jnp.concatenate([own_params, swap_cores(own_params)], axis=0)
    away = [
        lax.ppermute(params, "section", [(i, i ^ (2 * offset)) for i in range(8)])
        for offset in (1, 2, 3)
    ]
    params = jnp.concatenate([params] + away, axis=0)
    params = turn_params(params).reshape(sections * 8, TAPS)

    picked = pick(sec, slab_rows)
    moved = lax.all_to_all(
        picked.reshape(64, WIDE, TAPS), ("x", "quarter", "slot"), split_axis=0, concat_axis=0, tiled=True
    )
    outputs, states = chain(where, moved, params, sections)
    pieces = lax.all_to_all(
        outputs.reshape(sections * 16, WIDE, TAPS),
        ("section", "x", "slot"),
        split_axis=0,
        concat_axis=0,
        tiled=True,
    )

    info = lag_info(where, moved, states)
    local = jnp.where(section // 2 == quarter, info[0], jnp.zeros_like(info[0]))
    info = local + home_round(info[1], 1) + home_round(info[2], 2) + home_round(info[3], 3)
    odd = (section & 1) != 0
    mine = jnp.where(odd, info[1], info[0])
    partner = swap_cores(jnp.where(odd, info[0], info[1]))
    info = jnp.where(odd, jnp.concatenate([partner, mine]), jnp.concatenate([mine, partner]))
    before = info[:, :GROUP, ::-1]
    last = info[:, GROUP:EDGE, ::-1]
    lags = jnp.sum(info[:, EDGE : EDGE + 3].astype(jnp.float32), axis=1)
    running = jnp.einsum(
        "gci,gcl->gil", last, jnp.concatenate([last, before], axis=2),
        preferred_element_type=jnp.float32,
    )
    is_last = (jnp.arange(TAPS) == TAPS - 1)[None, :, None]
    running = running + jnp.where(is_last, jnp.pad(lags, ((0, 0), (TAPS - 1, 1)))[:, None], 0.0)
    offset = 1
    while offset < TAPS:
        running = running + jnp.pad(
            running[:, offset:, offset:], ((0, 0), (0, offset), (0, offset))
        )
        offset = offset * 2
    upper = running[:, :, :TAPS]
    ahead = jnp.arange(TAPS)[None, :] >= jnp.arange(TAPS)[:, None]
    hessians = jnp.where(ahead[None], upper, jnp.swapaxes(upper, 1, 2))
    hessians = hessians * (2.0 / (64 * TAPS * GROUP))

    restored = place(pieces.reshape(sections, 4, 4, WIDE, TAPS))
    return (restored[None], hessians[None])


def solution(mesh):
    split = Mesh(mesh.devices.reshape(8, 4, QUARTERS, 4), EVERY)
    seq = ("x", "quarter", "slot")
    in_specs = (P(seq, None), P("section", seq, None), P("section", seq))
    out_specs = (P("section", seq, None), P("section", seq, None, None))
    return jax.shard_map(
        per_device, mesh=split, in_specs=in_specs, out_specs=out_specs, check_vma=False
    )
```

```python
import jax
import jax.numpy as jnp
from jax import lax
from jax.experimental import pallas as pl
from jax.experimental.pallas import tpu as pltpu
from jax.sharding import Mesh, PartitionSpec as P

GROUP = 16
TAPS = 128
QUARTERS = 4
WIDE = 32
SPAN = 256
SERVED = 4
HALO = 8
EDGE = 2 * GROUP
INFO = EDGE + 16
MIB = 1024 * 1024
EVERY = ("section", "x", "quarter", "slot")


def limits(mib):
    return pltpu.CompilerParams(vmem_limit_bytes=mib * MIB)


def pick_kernel(sec_ref, slab_ref, out_ref, held, turned, sems, out_sems):
    sec = sec_ref[0]
    copies = []
    for x in range(4):
        start = pl.multiple_of(x * 1024 + (sec // 2) * SPAN, SPAN)
        copies.append(pltpu.make_async_copy(slab_ref.at[:, pl.ds(start, SPAN)], held.at[x], sems.at[x]))
        copies[-1].start()
    rows = SPAN // 2
    out_row = lax.broadcasted_iota(jnp.int32, (rows, SPAN), 0)
    lane = lax.broadcasted_iota(jnp.int32, (rows, SPAN), 1)
    wanted = (out_row // WIDE) * 64 + (sec % 2) * WIDE + out_row % WIDE
    chosen = jnp.where(lane == wanted, 1.0, 0.0).astype(jnp.bfloat16)
    for x in range(4):
        copies[x].wait()
        turned[x] = lax.dot_general(
            chosen, held[x], (((1,), (1,)), ((), ())), preferred_element_type=jnp.float32
        ).astype(jnp.bfloat16)
        for quarter in range(QUARTERS):
            place_at = x * QUARTERS + quarter
            copies.append(
                pltpu.make_async_copy(turned.at[x], out_ref.at[place_at], out_sems.at[place_at])
            )
            copies[-1].start()
    for copy in copies[4:]:
        copy.wait()


def pick(sec, slab_rows):
    length = slab_rows.shape[0]
    return pl.pallas_call(
        pick_kernel,
        in_specs=[pl.BlockSpec(memory_space=pltpu.SMEM), pl.BlockSpec(memory_space=pl.ANY)],
        out_specs=pl.BlockSpec(memory_space=pl.ANY),
        out_shape=jax.ShapeDtypeStruct((4 * QUARTERS, SPAN // 2, length), jnp.bfloat16),
        scratch_shapes=[
            pltpu.VMEM((4, length, SPAN), jnp.bfloat16),
            pltpu.VMEM((4, SPAN // 2, length), jnp.bfloat16),
            pltpu.SemaphoreType.DMA((4,)),
            pltpu.SemaphoreType.DMA((4 * QUARTERS,)),
        ],
        name="pick",
    )(sec, slab_rows)


def section_params(step, sec, quarter, par):
    lane = lax.broadcasted_iota(jnp.int32, (GROUP, TAPS), 1)
    chan = lax.broadcasted_iota(jnp.int32, (GROUP, TAPS), 0)
    slot = 2 * ((step // 2) ^ quarter) + ((step % 2) ^ (sec % 2))
    skip_row = jnp.broadcast_to(par[pl.ds(slot * 8 + 4, 1), :], (GROUP, TAPS))
    bands, gains = [], []
    for part in range(WIDE // GROUP):
        taps_row = par[pl.ds(slot * 8 + 2 * (sec % 2) + part, 1), :]
        spread = jnp.concatenate([taps_row, jnp.zeros_like(taps_row)], axis=1)
        spread = jnp.broadcast_to(spread, (TAPS, 2 * TAPS))
        bands.append(pltpu.roll(spread, 0, 1, stride=1, stride_axis=0).astype(jnp.bfloat16))
        own = jnp.where(lane == (sec % 2) * WIDE + part * GROUP + chan, skip_row, 0.0)
        gains.append(jnp.broadcast_to(jnp.sum(own, axis=1, keepdims=True), (GROUP, TAPS)))
    return bands, gains


def serve_kernel(where_ref, x_ref, par_ref, out_ref, par, state, sems):
    sec = where_ref[0]
    quarter = where_ref[1]
    sections = out_ref.shape[0]
    reach = HALO + SERVED
    par[...] = par_ref[...].astype(jnp.float32)

    for ahead in range(HALO // SERVED):

        @pl.when(quarter == ahead)
        def _():
            missing = HALO - SERVED * ahead
            state[0, 0, :missing] = jnp.zeros((missing, WIDE, TAPS), jnp.bfloat16)
            state[0, 0, missing:] = x_ref[: reach - missing]

    @pl.when(quarter >= HALO // SERVED)
    def _():
        state[0, 0] = x_ref[pl.ds(SERVED * quarter - HALO, reach)]

    for x in range(1, 4):
        state[0, x] = x_ref[pl.ds(16 * x + SERVED * quarter - HALO, reach)]

    copies = []
    for step in range(sections):
        bands, gains = section_params(step, sec, quarter, par)
        count = reach - step
        for x in range(4):
            for part in range(WIDE // GROUP):
                low = part * GROUP
                current = state[step, x, step:, low : low + GROUP, :].reshape(count * GROUP, TAPS)
                both = jnp.dot(current, bands[part], preferred_element_type=jnp.float32)
                direct = current[GROUP:].astype(jnp.float32).reshape(count - 1, GROUP, TAPS)
                direct = (direct * gains[part][None]).reshape((count - 1) * GROUP, TAPS)
                filtered = both[GROUP:, :TAPS] + both[:-GROUP, TAPS:] + direct
                state[step + 1, x, step + 1 :, low : low + GROUP, :] = filtered.astype(
                    jnp.bfloat16
                ).reshape(count - 1, GROUP, TAPS)
            copies.append(
                pltpu.make_async_copy(
                    state.at[step + 1, x, pl.ds(HALO, SERVED)], out_ref.at[step, x], sems.at[step, x]
                )
            )
            copies[-1].start()
    for copy in copies:
        copy.wait()


def serve(where, rows_in, params, sections):
    return pl.pallas_call(
        serve_kernel,
        in_specs=[pl.BlockSpec(memory_space=pltpu.SMEM)] + [pl.BlockSpec(memory_space=pltpu.VMEM)] * 2,
        out_specs=pl.BlockSpec(memory_space=pl.ANY),
        out_shape=jax.ShapeDtypeStruct((sections, 4, SERVED, WIDE, TAPS), jnp.bfloat16),
        scratch_shapes=[
            pltpu.VMEM(params.shape, jnp.float32),
            pltpu.VMEM((sections + 1, 4, HALO + SERVED, WIDE, TAPS), jnp.bfloat16),
            pltpu.SemaphoreType.DMA((sections, 4)),
        ],
        compiler_params=limits(24),
        name="serve",
    )(where, rows_in, params)


def lags_kernel(where_ref, x_ref, par_ref, info_ref, par, y_ref):
    sec = where_ref[0]
    quarter = where_ref[1]
    share = 16
    sections, blocks = y_ref.shape[0] + 1, y_ref.shape[1]
    rows = (blocks - 1) * GROUP
    blank = jnp.zeros((GROUP, TAPS), jnp.bfloat16)
    par[...] = par_ref[...].astype(jnp.float32)
    for step in range(sections):
        bands, gains = section_params(step, sec, quarter, par)
        slot = (step // 2) ^ quarter
        for part in range(WIDE // GROUP):
            low = part * GROUP
            if step == 0:
                whole = x_ref[:, low : low + GROUP, :]
            else:
                whole = y_ref[step - 1, :, low : low + GROUP, :]
            carry = jnp.zeros((GROUP, TAPS), jnp.float32)
            for first in range(0, blocks if step + 1 < sections else 0, share):
                current = whole[first : first + share].reshape(share * GROUP, TAPS)
                both = jnp.dot(current, bands[part], preferred_element_type=jnp.float32)
                carried = jnp.concatenate([carry, both[: (share - 1) * GROUP, TAPS:]], axis=0)
                carry = both[(share - 1) * GROUP :, TAPS:]
                direct = current.astype(jnp.float32).reshape(share, GROUP, TAPS) * gains[part][None]
                filtered = both[:, :TAPS] + carried + direct.reshape(share * GROUP, TAPS)
                y_ref[step, first : first + share, low : low + GROUP, :] = filtered.astype(
                    jnp.bfloat16
                ).reshape(share, GROUP, TAPS)
            body = whole[: blocks - 1].reshape(rows, TAPS)
            after = jnp.concatenate([body[GROUP:], blank], axis=0)
            pair = jnp.concatenate([body, after], axis=1)
            gram = lax.dot_general(
                body, pair, (((0,), (0,)), ((), ())), preferred_element_type=jnp.float32
            )
            size = TAPS
            while size > 8:
                size = size // 2
                gram = gram[:size] + pltpu.roll(gram[size:], 2 * TAPS - size, 1)
            row = lax.broadcasted_iota(jnp.int32, gram.shape, 0)
            for bit in (4, 2, 1):
                gram = jnp.where((row & bit) != 0, pltpu.roll(gram, 2 * TAPS - bit, 1), gram)
            lags = jnp.sum(gram, axis=0, keepdims=True)[:, :TAPS]
            high = lags.astype(jnp.bfloat16).astype(jnp.float32)
            middle = (lags - high).astype(jnp.bfloat16).astype(jnp.float32)
            rest = lags - high - middle
            info_row = lax.broadcasted_iota(jnp.int32, (INFO - EDGE, TAPS), 0)
            packed = jnp.where(
                info_row == 0,
                high,
                jnp.where(info_row == 1, middle, jnp.where(info_row == 2, rest, 0.0)),
            )
            edge = whole[blocks - 2 :].reshape(EDGE, TAPS)
            piece = jnp.concatenate([edge, packed.astype(jnp.bfloat16)], axis=0)
            info_ref[slot, step % 2, part] = piece


def lag_info(where, rows_in, params, sections):
    blocks = rows_in.shape[0]
    return pl.pallas_call(
        lags_kernel,
        in_specs=[pl.BlockSpec(memory_space=pltpu.SMEM)] + [pl.BlockSpec(memory_space=pltpu.VMEM)] * 2,
        out_specs=pl.BlockSpec(memory_space=pltpu.VMEM),
        out_shape=jax.ShapeDtypeStruct((sections // 2, 2, WIDE // GROUP, INFO, TAPS), jnp.bfloat16),
        scratch_shapes=[
            pltpu.VMEM(params.shape, jnp.float32),
            pltpu.VMEM((sections - 1, blocks, WIDE, TAPS), jnp.bfloat16),
        ],
        compiler_params=limits(24),
        cost_estimate=pl.CostEstimate(
            flops=8 * sections * rows_in.size * TAPS,
            bytes_accessed=4 * sections * rows_in.size,
            transcendentals=0,
        ),
        name="lags",
    )(where, rows_in, params)


def place_kernel(x_ref, out_ref, turned, sems):
    copies = []
    for x in range(4):
        for fourth in range(4):
            for pair in range(2):
                parts = [
                    x_ref[2 * fourth + half, x, 2 * pair + slot]
                    for slot in range(2)
                    for half in range(2)
                ]
                tile = jnp.concatenate(parts, axis=0)
                at = 1024 * x + SPAN * fourth + TAPS * pair
                turned[:, at : at + TAPS] = tile.T
        span = pl.ds(x * 1024, 1024)
        copies.append(pltpu.make_async_copy(turned.at[:, span], out_ref.at[:, span], sems.at[x]))
        copies[-1].start()
    for copy in copies:
        copy.wait()


def place(pieces):
    width = pieces.size // TAPS
    return pl.pallas_call(
        place_kernel,
        in_specs=[pl.BlockSpec(memory_space=pltpu.VMEM)],
        out_specs=pl.BlockSpec(memory_space=pl.ANY),
        out_shape=jax.ShapeDtypeStruct((TAPS, width), jnp.bfloat16),
        scratch_shapes=[pltpu.VMEM((TAPS, width), jnp.bfloat16), pltpu.SemaphoreType.DMA((4,))],
        compiler_params=limits(16),
        name="place",
    )(pieces)


def device(section, x, quarter, slot):
    return ((section * 4 + x) * QUARTERS + quarter) * 4 + slot


def turn_params(value):
    pairs = []
    for x in range(4):
        for slot in range(4):
            for quarter in range(QUARTERS):
                for chip in range(4):
                    for core in range(2):
                        origin = device(2 * chip + core, x, quarter, slot)
                        pairs.append((origin, device(2 * quarter + core, x, chip, slot)))
    return lax.ppermute(value, EVERY, pairs)


def home_round(value, offset):
    pairs = []
    for x in range(4):
        for slot in range(4):
            for quarter in range(QUARTERS):
                for core in range(2):
                    origin = device(2 * quarter + core, x, quarter, slot)
                    pairs.append((origin, device(2 * (quarter ^ offset) + core, x, quarter, slot)))
    return lax.ppermute(value, EVERY, pairs)


def swap_cores(value):
    return lax.ppermute(value, "section", [(i, i ^ 1) for i in range(8)])


def per_device(slab_rows, filter_taps, skip_weights):
    sections = lax.axis_size("section")
    section = lax.axis_index("section").astype(jnp.int32)
    quarter = lax.axis_index("quarter").astype(jnp.int32)
    sec = section.reshape(1)
    where = jnp.stack([section, quarter])

    own_params = jnp.concatenate(
        [filter_taps[0], jnp.pad(skip_weights, ((0, 3), (0, TAPS - skip_weights.shape[1])))], axis=0
    )[None]
    params = jnp.concatenate([own_params, swap_cores(own_params)], axis=0)
    away = [
        lax.ppermute(params, "section", [(i, i ^ (2 * offset)) for i in range(8)])
        for offset in (1, 2, 3)
    ]
    params = jnp.concatenate([params] + away, axis=0)
    params = turn_params(params).reshape(sections * 8, TAPS)

    picked = pick(sec, slab_rows)
    moved = lax.all_to_all(
        picked.reshape(64, WIDE, TAPS), ("x", "quarter", "slot"), split_axis=0, concat_axis=0, tiled=True
    )
    outputs = serve(where, moved, params, sections)
    pieces = lax.all_to_all(
        outputs.reshape(sections * 16, WIDE, TAPS),
        ("section", "x", "slot"),
        split_axis=0,
        concat_axis=0,
        tiled=True,
    )

    info = lag_info(where, moved, params, sections)
    local = jnp.where(section // 2 == quarter, info[0], jnp.zeros_like(info[0]))
    info = local + home_round(info[1], 1) + home_round(info[2], 2) + home_round(info[3], 3)
    odd = (section & 1) != 0
    mine = jnp.where(odd, info[1], info[0])
    partner = swap_cores(jnp.where(odd, info[0], info[1]))
    info = jnp.where(odd, jnp.concatenate([partner, mine]), jnp.concatenate([mine, partner]))
    before = info[:, :GROUP, ::-1]
    last = info[:, GROUP:EDGE, ::-1]
    lags = jnp.sum(info[:, EDGE : EDGE + 3].astype(jnp.float32), axis=1)
    running = jnp.einsum(
        "gci,gcl->gil", last, jnp.concatenate([last, before], axis=2),
        preferred_element_type=jnp.float32,
    )
    is_last = (jnp.arange(TAPS) == TAPS - 1)[None, :, None]
    running = running + jnp.where(is_last, jnp.pad(lags, ((0, 0), (TAPS - 1, 1)))[:, None], 0.0)
    offset = 1
    while offset < TAPS:
        running = running + jnp.pad(
            running[:, offset:, offset:], ((0, 0), (0, offset), (0, offset))
        )
        offset = offset * 2
    upper = running[:, :, :TAPS]
    ahead = jnp.arange(TAPS)[None, :] >= jnp.arange(TAPS)[:, None]
    hessians = jnp.where(ahead[None], upper, jnp.swapaxes(upper, 1, 2))
    hessians = hessians * (2.0 / (64 * TAPS * GROUP))

    restored = place(pieces.reshape(sections, 4, 4, WIDE, TAPS))
    return (restored[None], hessians[None])


def solution(mesh):
    split = Mesh(mesh.devices.reshape(8, 4, QUARTERS, 4), EVERY)
    seq = ("x", "quarter", "slot")
    in_specs = (P(seq, None), P("section", seq, None), P("section", seq))
    out_specs = (P("section", seq, None), P("section", seq, None, None))
    return jax.shard_map(
        per_device, mesh=split, in_specs=in_specs, out_specs=out_specs, check_vma=False
    )
```

```python
import jax
import jax.numpy as jnp
from jax import lax
from jax.experimental import pallas as pl
from jax.experimental.pallas import tpu as pltpu
from jax.sharding import Mesh, PartitionSpec as P

GROUP = 16
TAPS = 128
QUARTERS = 4
WIDE = 32
SPAN = 256
SERVED = 4
HALO = 8
EDGE = 2 * GROUP
INFO = EDGE + 16
MIB = 1024 * 1024
EVERY = ("section", "x", "quarter", "slot")


def limits(mib):
    return pltpu.CompilerParams(vmem_limit_bytes=mib * MIB)


def pick_kernel(sec_ref, slab_ref, out_ref, held, turned, sems, out_sems):
    sec = sec_ref[0]
    copies = []
    for x in range(4):
        start = pl.multiple_of(x * 1024 + (sec // 2) * SPAN, SPAN)
        copies.append(pltpu.make_async_copy(slab_ref.at[:, pl.ds(start, SPAN)], held.at[x], sems.at[x]))
        copies[-1].start()
    rows = SPAN // 2
    out_row = lax.broadcasted_iota(jnp.int32, (rows, SPAN), 0)
    lane = lax.broadcasted_iota(jnp.int32, (rows, SPAN), 1)
    wanted = (out_row // WIDE) * 64 + (sec % 2) * WIDE + out_row % WIDE
    chosen = jnp.where(lane == wanted, 1.0, 0.0).astype(jnp.bfloat16)
    for x in range(4):
        copies[x].wait()
        turned[x] = lax.dot_general(
            chosen, held[x], (((1,), (1,)), ((), ())), preferred_element_type=jnp.float32
        ).astype(jnp.bfloat16)
        for quarter in range(QUARTERS):
            place_at = x * QUARTERS + quarter
            copies.append(
                pltpu.make_async_copy(turned.at[x], out_ref.at[place_at], out_sems.at[place_at])
            )
            copies[-1].start()
    for copy in copies[4:]:
        copy.wait()


def pick(sec, slab_rows):
    length = slab_rows.shape[0]
    return pl.pallas_call(
        pick_kernel,
        in_specs=[pl.BlockSpec(memory_space=pltpu.SMEM), pl.BlockSpec(memory_space=pl.ANY)],
        out_specs=pl.BlockSpec(memory_space=pl.ANY),
        out_shape=jax.ShapeDtypeStruct((4 * QUARTERS, SPAN // 2, length), jnp.bfloat16),
        scratch_shapes=[
            pltpu.VMEM((4, length, SPAN), jnp.bfloat16),
            pltpu.VMEM((4, SPAN // 2, length), jnp.bfloat16),
            pltpu.SemaphoreType.DMA((4,)),
            pltpu.SemaphoreType.DMA((4 * QUARTERS,)),
        ],
        name="pick",
    )(sec, slab_rows)


def section_params(step, sec, quarter, par):
    lane = lax.broadcasted_iota(jnp.int32, (GROUP, TAPS), 1)
    chan = lax.broadcasted_iota(jnp.int32, (GROUP, TAPS), 0)
    slot = 2 * ((step // 2) ^ quarter) + ((step % 2) ^ (sec % 2))
    skip_row = jnp.broadcast_to(par[pl.ds(slot * 8 + 4, 1), :], (GROUP, TAPS))
    bands, gains = [], []
    for part in range(WIDE // GROUP):
        taps_row = par[pl.ds(slot * 8 + 2 * (sec % 2) + part, 1), :]
        spread = jnp.concatenate([taps_row, jnp.zeros_like(taps_row)], axis=1)
        spread = jnp.broadcast_to(spread, (TAPS, 2 * TAPS))
        bands.append(pltpu.roll(spread, 0, 1, stride=1, stride_axis=0).astype(jnp.bfloat16))
        own = jnp.where(lane == (sec % 2) * WIDE + part * GROUP + chan, skip_row, 0.0)
        gains.append(jnp.broadcast_to(jnp.sum(own, axis=1, keepdims=True), (GROUP, TAPS)))
    return bands, gains


def serve_kernel(where_ref, x_ref, par_ref, out_ref, par, state, sems):
    sec = where_ref[0]
    quarter = where_ref[1]
    sections = out_ref.shape[0]
    reach = HALO + SERVED
    par[...] = par_ref[...].astype(jnp.float32)

    for ahead in range(HALO // SERVED):

        @pl.when(quarter == ahead)
        def _():
            missing = HALO - SERVED * ahead
            state[0, 0, :missing] = jnp.zeros((missing, WIDE, TAPS), jnp.bfloat16)
            state[0, 0, missing:] = x_ref[: reach - missing]

    @pl.when(quarter >= HALO // SERVED)
    def _():
        state[0, 0] = x_ref[pl.ds(SERVED * quarter - HALO, reach)]

    for x in range(1, 4):
        state[0, x] = x_ref[pl.ds(16 * x + SERVED * quarter - HALO, reach)]

    copies = []
    for step in range(sections):
        bands, gains = section_params(step, sec, quarter, par)
        count = reach - step
        for part in range(WIDE // GROUP):
            low = part * GROUP
            current = state[step, :, step:, low : low + GROUP, :]
            both = jnp.dot(
                current.reshape(4 * count * GROUP, TAPS), bands[part], preferred_element_type=jnp.float32
            ).reshape(4, count, GROUP, 2 * TAPS)
            direct = current[:, 1:].astype(jnp.float32) * gains[part][None, None]
            filtered = both[:, 1:, :, :TAPS] + both[:, :-1, :, TAPS:] + direct
            state[step + 1, :, step + 1 :, low : low + GROUP, :] = filtered.astype(jnp.bfloat16)
        copies.append(
            pltpu.make_async_copy(
                state.at[step + 1, :, pl.ds(HALO, SERVED)], out_ref.at[step], sems.at[step]
            )
        )
        copies[-1].start()
    for copy in copies:
        copy.wait()


def serve(where, rows_in, params, sections):
    return pl.pallas_call(
        serve_kernel,
        in_specs=[pl.BlockSpec(memory_space=pltpu.SMEM)] + [pl.BlockSpec(memory_space=pltpu.VMEM)] * 2,
        out_specs=pl.BlockSpec(memory_space=pl.ANY),
        out_shape=jax.ShapeDtypeStruct((sections, 4, SERVED, WIDE, TAPS), jnp.bfloat16),
        scratch_shapes=[
            pltpu.VMEM(params.shape, jnp.float32),
            pltpu.VMEM((sections + 1, 4, HALO + SERVED, WIDE, TAPS), jnp.bfloat16),
            pltpu.SemaphoreType.DMA((sections,)),
        ],
        compiler_params=limits(24),
        name="serve",
    )(where, rows_in, params)


def lags_kernel(where_ref, x_ref, par_ref, info_ref, par, y_ref):
    sec = where_ref[0]
    quarter = where_ref[1]
    share = 16
    sections, blocks = y_ref.shape[0] + 1, y_ref.shape[1]
    rows = (blocks - 1) * GROUP
    blank = jnp.zeros((GROUP, TAPS), jnp.bfloat16)
    par[...] = par_ref[...].astype(jnp.float32)
    for step in range(sections):
        bands, gains = section_params(step, sec, quarter, par)
        slot = (step // 2) ^ quarter
        for part in range(WIDE // GROUP):
            low = part * GROUP
            if step == 0:
                whole = x_ref[:, low : low + GROUP, :]
            else:
                whole = y_ref[step - 1, :, low : low + GROUP, :]
            carry = jnp.zeros((GROUP, TAPS), jnp.float32)
            for first in range(0, blocks if step + 1 < sections else 0, share):
                current = whole[first : first + share].reshape(share * GROUP, TAPS)
                both = jnp.dot(current, bands[part], preferred_element_type=jnp.float32)
                carried = jnp.concatenate([carry, both[: (share - 1) * GROUP, TAPS:]], axis=0)
                carry = both[(share - 1) * GROUP :, TAPS:]
                direct = current.astype(jnp.float32).reshape(share, GROUP, TAPS) * gains[part][None]
                filtered = both[:, :TAPS] + carried + direct.reshape(share * GROUP, TAPS)
                y_ref[step, first : first + share, low : low + GROUP, :] = filtered.astype(
                    jnp.bfloat16
                ).reshape(share, GROUP, TAPS)
            body = whole[: blocks - 1].reshape(rows, TAPS)
            after = jnp.concatenate([body[GROUP:], blank], axis=0)
            pair = jnp.concatenate([body, after], axis=1)
            gram = lax.dot_general(
                body, pair, (((0,), (0,)), ((), ())), preferred_element_type=jnp.float32
            )
            size = TAPS
            while size > 8:
                size = size // 2
                gram = gram[:size] + pltpu.roll(gram[size:], 2 * TAPS - size, 1)
            row = lax.broadcasted_iota(jnp.int32, gram.shape, 0)
            for bit in (4, 2, 1):
                gram = jnp.where((row & bit) != 0, pltpu.roll(gram, 2 * TAPS - bit, 1), gram)
            lags = jnp.sum(gram, axis=0, keepdims=True)[:, :TAPS]
            high = lags.astype(jnp.bfloat16).astype(jnp.float32)
            middle = (lags - high).astype(jnp.bfloat16).astype(jnp.float32)
            rest = lags - high - middle
            info_row = lax.broadcasted_iota(jnp.int32, (INFO - EDGE, TAPS), 0)
            packed = jnp.where(
                info_row == 0,
                high,
                jnp.where(info_row == 1, middle, jnp.where(info_row == 2, rest, 0.0)),
            )
            edge = whole[blocks - 2 :].reshape(EDGE, TAPS)
            piece = jnp.concatenate([edge, packed.astype(jnp.bfloat16)], axis=0)
            info_ref[slot, step % 2, part] = piece


def lag_info(where, rows_in, params, sections):
    blocks = rows_in.shape[0]
    return pl.pallas_call(
        lags_kernel,
        in_specs=[pl.BlockSpec(memory_space=pltpu.SMEM)] + [pl.BlockSpec(memory_space=pltpu.VMEM)] * 2,
        out_specs=pl.BlockSpec(memory_space=pltpu.VMEM),
        out_shape=jax.ShapeDtypeStruct((sections // 2, 2, WIDE // GROUP, INFO, TAPS), jnp.bfloat16),
        scratch_shapes=[
            pltpu.VMEM(params.shape, jnp.float32),
            pltpu.VMEM((sections - 1, blocks, WIDE, TAPS), jnp.bfloat16),
        ],
        compiler_params=limits(24),
        cost_estimate=pl.CostEstimate(
            flops=8 * sections * rows_in.size * TAPS,
            bytes_accessed=4 * sections * rows_in.size,
            transcendentals=0,
        ),
        name="lags",
    )(where, rows_in, params)


def place_kernel(x_ref, out_ref, turned, sems):
    copies = []
    for x in range(4):
        for fourth in range(4):
            for pair in range(2):
                parts = [
                    x_ref[2 * fourth + half, x, 2 * pair + slot]
                    for slot in range(2)
                    for half in range(2)
                ]
                tile = jnp.concatenate(parts, axis=0)
                at = 1024 * x + SPAN * fourth + TAPS * pair
                turned[:, at : at + TAPS] = tile.T
        span = pl.ds(x * 1024, 1024)
        copies.append(pltpu.make_async_copy(turned.at[:, span], out_ref.at[:, span], sems.at[x]))
        copies[-1].start()
    for copy in copies:
        copy.wait()


def place(pieces):
    width = pieces.size // TAPS
    return pl.pallas_call(
        place_kernel,
        in_specs=[pl.BlockSpec(memory_space=pltpu.VMEM)],
        out_specs=pl.BlockSpec(memory_space=pl.ANY),
        out_shape=jax.ShapeDtypeStruct((TAPS, width), jnp.bfloat16),
        scratch_shapes=[pltpu.VMEM((TAPS, width), jnp.bfloat16), pltpu.SemaphoreType.DMA((4,))],
        compiler_params=limits(16),
        name="place",
    )(pieces)


def device(section, x, quarter, slot):
    return ((section * 4 + x) * QUARTERS + quarter) * 4 + slot


def turn_params(value):
    pairs = []
    for x in range(4):
        for slot in range(4):
            for quarter in range(QUARTERS):
                for chip in range(4):
                    for core in range(2):
                        origin = device(2 * chip + core, x, quarter, slot)
                        pairs.append((origin, device(2 * quarter + core, x, chip, slot)))
    return lax.ppermute(value, EVERY, pairs)


def home_round(value, offset):
    pairs = []
    for x in range(4):
        for slot in range(4):
            for quarter in range(QUARTERS):
                for core in range(2):
                    origin = device(2 * quarter + core, x, quarter, slot)
                    pairs.append((origin, device(2 * (quarter ^ offset) + core, x, quarter, slot)))
    return lax.ppermute(value, EVERY, pairs)


def swap_cores(value):
    return lax.ppermute(value, "section", [(i, i ^ 1) for i in range(8)])


def per_device(slab_rows, filter_taps, skip_weights):
    sections = lax.axis_size("section")
    section = lax.axis_index("section").astype(jnp.int32)
    quarter = lax.axis_index("quarter").astype(jnp.int32)
    sec = section.reshape(1)
    where = jnp.stack([section, quarter])

    own_params = jnp.concatenate(
        [filter_taps[0], jnp.pad(skip_weights, ((0, 3), (0, TAPS - skip_weights.shape[1])))], axis=0
    )[None]
    params = jnp.concatenate([own_params, swap_cores(own_params)], axis=0)
    away = [
        lax.ppermute(params, "section", [(i, i ^ (2 * offset)) for i in range(8)])
        for offset in (1, 2, 3)
    ]
    params = jnp.concatenate([params] + away, axis=0)
    params = turn_params(params).reshape(sections * 8, TAPS)

    picked = pick(sec, slab_rows)
    moved = lax.all_to_all(
        picked.reshape(64, WIDE, TAPS), ("x", "quarter", "slot"), split_axis=0, concat_axis=0, tiled=True
    )
    outputs = serve(where, moved, params, sections)
    pieces = lax.all_to_all(
        outputs.reshape(sections * 16, WIDE, TAPS),
        ("section", "x", "slot"),
        split_axis=0,
        concat_axis=0,
        tiled=True,
    )

    info = lag_info(where, moved, params, sections)
    local = jnp.where(section // 2 == quarter, info[0], jnp.zeros_like(info[0]))
    info = local + home_round(info[1], 1) + home_round(info[2], 2) + home_round(info[3], 3)
    odd = (section & 1) != 0
    mine = jnp.where(odd, info[1], info[0])
    partner = swap_cores(jnp.where(odd, info[0], info[1]))
    info = jnp.where(odd, jnp.concatenate([partner, mine]), jnp.concatenate([mine, partner]))
    before = info[:, :GROUP, ::-1]
    last = info[:, GROUP:EDGE, ::-1]
    lags = jnp.sum(info[:, EDGE : EDGE + 3].astype(jnp.float32), axis=1)
    running = jnp.einsum(
        "gci,gcl->gil", last, jnp.concatenate([last, before], axis=2),
        preferred_element_type=jnp.float32,
    )
    is_last = (jnp.arange(TAPS) == TAPS - 1)[None, :, None]
    running = running + jnp.where(is_last, jnp.pad(lags, ((0, 0), (TAPS - 1, 1)))[:, None], 0.0)
    offset = 1
    while offset < TAPS:
        running = running + jnp.pad(
            running[:, offset:, offset:], ((0, 0), (0, offset), (0, offset))
        )
        offset = offset * 2
    upper = running[:, :, :TAPS]
    ahead = jnp.arange(TAPS)[None, :] >= jnp.arange(TAPS)[:, None]
    hessians = jnp.where(ahead[None], upper, jnp.swapaxes(upper, 1, 2))
    hessians = hessians * (2.0 / (64 * TAPS * GROUP))

    restored = place(pieces.reshape(sections, 4, 4, WIDE, TAPS))
    return (restored[None], hessians[None])


def solution(mesh):
    split = Mesh(mesh.devices.reshape(8, 4, QUARTERS, 4), EVERY)
    seq = ("x", "quarter", "slot")
    in_specs = (P(seq, None), P("section", seq, None), P("section", seq))
    out_specs = (P("section", seq, None), P("section", seq, None, None))
    return jax.shard_map(
        per_device, mesh=split, in_specs=in_specs, out_specs=out_specs, check_vma=False
    )
```

```python
import jax
import jax.numpy as jnp
from jax import lax
from jax.experimental import pallas as pl
from jax.experimental.pallas import tpu as pltpu
from jax.sharding import Mesh, PartitionSpec as P

GROUP = 16
TAPS = 128
QUARTERS = 4
WIDE = 32
SPAN = 256
SERVED = 4
HALO = 8
EDGE = 2 * GROUP
INFO = EDGE + 16
MIB = 1024 * 1024
EVERY = ("section", "x", "quarter", "slot")


def limits(mib):
    return pltpu.CompilerParams(vmem_limit_bytes=mib * MIB)


def pick_kernel(sec_ref, slab_ref, out_ref, held, turned, sems, out_sems):
    sec = sec_ref[0]
    copies = []
    for x in range(4):
        start = pl.multiple_of(x * 1024 + (sec // 2) * SPAN, SPAN)
        copies.append(pltpu.make_async_copy(slab_ref.at[:, pl.ds(start, SPAN)], held.at[x], sems.at[x]))
        copies[-1].start()
    rows = SPAN // 2
    out_row = lax.broadcasted_iota(jnp.int32, (rows, SPAN), 0)
    lane = lax.broadcasted_iota(jnp.int32, (rows, SPAN), 1)
    wanted = (out_row // WIDE) * 64 + (sec % 2) * WIDE + out_row % WIDE
    chosen = jnp.where(lane == wanted, 1.0, 0.0).astype(jnp.bfloat16)
    for x in range(4):
        copies[x].wait()
        turned[x] = lax.dot_general(
            chosen, held[x], (((1,), (1,)), ((), ())), preferred_element_type=jnp.float32
        ).astype(jnp.bfloat16)
        for quarter in range(QUARTERS):
            place_at = x * QUARTERS + quarter
            copies.append(
                pltpu.make_async_copy(turned.at[x], out_ref.at[place_at], out_sems.at[place_at])
            )
            copies[-1].start()
    for copy in copies[4:]:
        copy.wait()


def pick(sec, slab_rows):
    length = slab_rows.shape[0]
    return pl.pallas_call(
        pick_kernel,
        in_specs=[pl.BlockSpec(memory_space=pltpu.SMEM), pl.BlockSpec(memory_space=pl.ANY)],
        out_specs=pl.BlockSpec(memory_space=pl.ANY),
        out_shape=jax.ShapeDtypeStruct((4 * QUARTERS, SPAN // 2, length), jnp.bfloat16),
        scratch_shapes=[
            pltpu.VMEM((4, length, SPAN), jnp.bfloat16),
            pltpu.VMEM((4, SPAN // 2, length), jnp.bfloat16),
            pltpu.SemaphoreType.DMA((4,)),
            pltpu.SemaphoreType.DMA((4 * QUARTERS,)),
        ],
        name="pick",
    )(sec, slab_rows)


def section_params(step, sec, quarter, par):
    lane = lax.broadcasted_iota(jnp.int32, (GROUP, TAPS), 1)
    chan = lax.broadcasted_iota(jnp.int32, (GROUP, TAPS), 0)
    slot = 2 * ((step // 2) ^ quarter) + ((step % 2) ^ (sec % 2))
    skip_row = jnp.broadcast_to(par[pl.ds(slot * 8 + 4, 1), :], (GROUP, TAPS))
    bands, gains = [], []
    for part in range(WIDE // GROUP):
        taps_row = par[pl.ds(slot * 8 + 2 * (sec % 2) + part, 1), :]
        spread = jnp.concatenate([taps_row, jnp.zeros_like(taps_row)], axis=1)
        spread = jnp.broadcast_to(spread, (TAPS, 2 * TAPS))
        bands.append(pltpu.roll(spread, 0, 1, stride=1, stride_axis=0).astype(jnp.bfloat16))
        own = jnp.where(lane == (sec % 2) * WIDE + part * GROUP + chan, skip_row, 0.0)
        gains.append(jnp.broadcast_to(jnp.sum(own, axis=1, keepdims=True), (GROUP, TAPS)))
    return bands, gains


def serve_kernel(where_ref, x_ref, par_ref, out_ref, par, state, sems):
    sec = where_ref[0]
    quarter = where_ref[1]
    sections = out_ref.shape[0]
    reach = HALO + SERVED
    par[...] = par_ref[...].astype(jnp.float32)

    for ahead in range(HALO // SERVED):

        @pl.when(quarter == ahead)
        def _():
            missing = HALO - SERVED * ahead
            state[0, 0, :missing] = jnp.zeros((missing, WIDE, TAPS), jnp.bfloat16)
            state[0, 0, missing:] = x_ref[: reach - missing]

    @pl.when(quarter >= HALO // SERVED)
    def _():
        state[0, 0] = x_ref[pl.ds(SERVED * quarter - HALO, reach)]

    for x in range(1, 4):
        state[0, x] = x_ref[pl.ds(16 * x + SERVED * quarter - HALO, reach)]

    copies = []
    ready = section_params(0, sec, quarter, par)
    for step in range(sections):
        bands, gains = ready
        if step + 1 < sections:
            ready = section_params(step + 1, sec, quarter, par)
        count = reach - step
        for part in range(WIDE // GROUP):
            low = part * GROUP
            current = state[step, :, step:, low : low + GROUP, :]
            both = jnp.dot(
                current.reshape(4 * count * GROUP, TAPS), bands[part], preferred_element_type=jnp.float32
            ).reshape(4, count, GROUP, 2 * TAPS)
            direct = current[:, 1:].astype(jnp.float32) * gains[part][None, None]
            filtered = both[:, 1:, :, :TAPS] + both[:, :-1, :, TAPS:] + direct
            state[step + 1, :, step + 1 :, low : low + GROUP, :] = filtered.astype(jnp.bfloat16)
        copies.append(
            pltpu.make_async_copy(
                state.at[step + 1, :, pl.ds(HALO, SERVED)], out_ref.at[step], sems.at[step]
            )
        )
        copies[-1].start()
    for copy in copies:
        copy.wait()


def serve(where, rows_in, params, sections):
    return pl.pallas_call(
        serve_kernel,
        in_specs=[pl.BlockSpec(memory_space=pltpu.SMEM)] + [pl.BlockSpec(memory_space=pltpu.VMEM)] * 2,
        out_specs=pl.BlockSpec(memory_space=pl.ANY),
        out_shape=jax.ShapeDtypeStruct((sections, 4, SERVED, WIDE, TAPS), jnp.bfloat16),
        scratch_shapes=[
            pltpu.VMEM(params.shape, jnp.float32),
            pltpu.VMEM((sections + 1, 4, HALO + SERVED, WIDE, TAPS), jnp.bfloat16),
            pltpu.SemaphoreType.DMA((sections,)),
        ],
        compiler_params=limits(24),
        name="serve",
    )(where, rows_in, params)


def lags_kernel(where_ref, x_ref, par_ref, info_ref, par, y_ref):
    sec = where_ref[0]
    quarter = where_ref[1]
    share = 16
    sections, blocks = y_ref.shape[0] + 1, y_ref.shape[1]
    rows = (blocks - 1) * GROUP
    blank = jnp.zeros((GROUP, TAPS), jnp.bfloat16)
    par[...] = par_ref[...].astype(jnp.float32)
    for step in range(sections):
        bands, gains = section_params(step, sec, quarter, par)
        slot = (step // 2) ^ quarter
        for part in range(WIDE // GROUP):
            low = part * GROUP
            if step == 0:
                whole = x_ref[:, low : low + GROUP, :]
            else:
                whole = y_ref[step - 1, :, low : low + GROUP, :]
            carry = jnp.zeros((GROUP, TAPS), jnp.float32)
            for first in range(0, blocks if step + 1 < sections else 0, share):
                current = whole[first : first + share].reshape(share * GROUP, TAPS)
                both = jnp.dot(current, bands[part], preferred_element_type=jnp.float32)
                carried = jnp.concatenate([carry, both[: (share - 1) * GROUP, TAPS:]], axis=0)
                carry = both[(share - 1) * GROUP :, TAPS:]
                direct = current.astype(jnp.float32).reshape(share, GROUP, TAPS) * gains[part][None]
                filtered = both[:, :TAPS] + carried + direct.reshape(share * GROUP, TAPS)
                y_ref[step, first : first + share, low : low + GROUP, :] = filtered.astype(
                    jnp.bfloat16
                ).reshape(share, GROUP, TAPS)
            body = whole[: blocks - 1].reshape(rows, TAPS)
            after = jnp.concatenate([body[GROUP:], blank], axis=0)
            pair = jnp.concatenate([body, after], axis=1)
            gram = lax.dot_general(
                body, pair, (((0,), (0,)), ((), ())), preferred_element_type=jnp.float32
            )
            size = TAPS
            while size > 8:
                size = size // 2
                gram = gram[:size] + pltpu.roll(gram[size:], 2 * TAPS - size, 1)
            row = lax.broadcasted_iota(jnp.int32, gram.shape, 0)
            for bit in (4, 2, 1):
                gram = jnp.where((row & bit) != 0, pltpu.roll(gram, 2 * TAPS - bit, 1), gram)
            lags = jnp.sum(gram, axis=0, keepdims=True)[:, :TAPS]
            high = lags.astype(jnp.bfloat16).astype(jnp.float32)
            middle = (lags - high).astype(jnp.bfloat16).astype(jnp.float32)
            rest = lags - high - middle
            info_row = lax.broadcasted_iota(jnp.int32, (INFO - EDGE, TAPS), 0)
            packed = jnp.where(
                info_row == 0,
                high,
                jnp.where(info_row == 1, middle, jnp.where(info_row == 2, rest, 0.0)),
            )
            edge = whole[blocks - 2 :].reshape(EDGE, TAPS)
            piece = jnp.concatenate([edge, packed.astype(jnp.bfloat16)], axis=0)
            info_ref[slot, step % 2, part] = piece


def lag_info(where, rows_in, params, sections):
    blocks = rows_in.shape[0]
    return pl.pallas_call(
        lags_kernel,
        in_specs=[pl.BlockSpec(memory_space=pltpu.SMEM)] + [pl.BlockSpec(memory_space=pltpu.VMEM)] * 2,
        out_specs=pl.BlockSpec(memory_space=pltpu.VMEM),
        out_shape=jax.ShapeDtypeStruct((sections // 2, 2, WIDE // GROUP, INFO, TAPS), jnp.bfloat16),
        scratch_shapes=[
            pltpu.VMEM(params.shape, jnp.float32),
            pltpu.VMEM((sections - 1, blocks, WIDE, TAPS), jnp.bfloat16),
        ],
        compiler_params=limits(24),
        cost_estimate=pl.CostEstimate(
            flops=8 * sections * rows_in.size * TAPS,
            bytes_accessed=4 * sections * rows_in.size,
            transcendentals=0,
        ),
        name="lags",
    )(where, rows_in, params)


def place_kernel(x_ref, out_ref, turned, sems):
    copies = []
    for x in range(4):
        for fourth in range(4):
            for pair in range(2):
                parts = [
                    x_ref[2 * fourth + half, x, 2 * pair + slot]
                    for slot in range(2)
                    for half in range(2)
                ]
                tile = jnp.concatenate(parts, axis=0)
                at = 1024 * x + SPAN * fourth + TAPS * pair
                turned[:, at : at + TAPS] = tile.T
        span = pl.ds(x * 1024, 1024)
        copies.append(pltpu.make_async_copy(turned.at[:, span], out_ref.at[:, span], sems.at[x]))
        copies[-1].start()
    for copy in copies:
        copy.wait()


def place(pieces):
    width = pieces.size // TAPS
    return pl.pallas_call(
        place_kernel,
        in_specs=[pl.BlockSpec(memory_space=pltpu.VMEM)],
        out_specs=pl.BlockSpec(memory_space=pl.ANY),
        out_shape=jax.ShapeDtypeStruct((TAPS, width), jnp.bfloat16),
        scratch_shapes=[pltpu.VMEM((TAPS, width), jnp.bfloat16), pltpu.SemaphoreType.DMA((4,))],
        compiler_params=limits(16),
        name="place",
    )(pieces)


def device(section, x, quarter, slot):
    return ((section * 4 + x) * QUARTERS + quarter) * 4 + slot


def turn_params(value):
    pairs = []
    for x in range(4):
        for slot in range(4):
            for quarter in range(QUARTERS):
                for chip in range(4):
                    for core in range(2):
                        origin = device(2 * chip + core, x, quarter, slot)
                        pairs.append((origin, device(2 * quarter + core, x, chip, slot)))
    return lax.ppermute(value, EVERY, pairs)


def home_round(value, offset):
    pairs = []
    for x in range(4):
        for slot in range(4):
            for quarter in range(QUARTERS):
                for core in range(2):
                    origin = device(2 * quarter + core, x, quarter, slot)
                    pairs.append((origin, device(2 * (quarter ^ offset) + core, x, quarter, slot)))
    return lax.ppermute(value, EVERY, pairs)


def swap_cores(value):
    return lax.ppermute(value, "section", [(i, i ^ 1) for i in range(8)])


def per_device(slab_rows, filter_taps, skip_weights):
    sections = lax.axis_size("section")
    section = lax.axis_index("section").astype(jnp.int32)
    quarter = lax.axis_index("quarter").astype(jnp.int32)
    sec = section.reshape(1)
    where = jnp.stack([section, quarter])

    own_params = jnp.concatenate(
        [filter_taps[0], jnp.pad(skip_weights, ((0, 3), (0, TAPS - skip_weights.shape[1])))], axis=0
    )[None]
    params = jnp.concatenate([own_params, swap_cores(own_params)], axis=0)
    away = [
        lax.ppermute(params, "section", [(i, i ^ (2 * offset)) for i in range(8)])
        for offset in (1, 2, 3)
    ]
    params = jnp.concatenate([params] + away, axis=0)
    params = turn_params(params).reshape(sections * 8, TAPS)

    picked = pick(sec, slab_rows)
    moved = lax.all_to_all(
        picked.reshape(64, WIDE, TAPS), ("x", "quarter", "slot"), split_axis=0, concat_axis=0, tiled=True
    )
    outputs = serve(where, moved, params, sections)
    pieces = lax.all_to_all(
        outputs.reshape(sections * 16, WIDE, TAPS),
        ("section", "x", "slot"),
        split_axis=0,
        concat_axis=0,
        tiled=True,
    )

    info = lag_info(where, moved, params, sections)
    local = jnp.where(section // 2 == quarter, info[0], jnp.zeros_like(info[0]))
    info = local + home_round(info[1], 1) + home_round(info[2], 2) + home_round(info[3], 3)
    odd = (section & 1) != 0
    mine = jnp.where(odd, info[1], info[0])
    partner = swap_cores(jnp.where(odd, info[0], info[1]))
    info = jnp.where(odd, jnp.concatenate([partner, mine]), jnp.concatenate([mine, partner]))
    before = info[:, :GROUP, ::-1]
    last = info[:, GROUP:EDGE, ::-1]
    lags = jnp.sum(info[:, EDGE : EDGE + 3].astype(jnp.float32), axis=1)
    running = jnp.einsum(
        "gci,gcl->gil", last, jnp.concatenate([last, before], axis=2),
        preferred_element_type=jnp.float32,
    )
    is_last = (jnp.arange(TAPS) == TAPS - 1)[None, :, None]
    running = running + jnp.where(is_last, jnp.pad(lags, ((0, 0), (TAPS - 1, 1)))[:, None], 0.0)
    offset = 1
    while offset < TAPS:
        running = running + jnp.pad(
            running[:, offset:, offset:], ((0, 0), (0, offset), (0, offset))
        )
        offset = offset * 2
    upper = running[:, :, :TAPS]
    ahead = jnp.arange(TAPS)[None, :] >= jnp.arange(TAPS)[:, None]
    hessians = jnp.where(ahead[None], upper, jnp.swapaxes(upper, 1, 2))
    hessians = hessians * (2.0 / (64 * TAPS * GROUP))

    restored = place(pieces.reshape(sections, 4, 4, WIDE, TAPS))
    return (restored[None], hessians[None])


def solution(mesh):
    split = Mesh(mesh.devices.reshape(8, 4, QUARTERS, 4), EVERY)
    seq = ("x", "quarter", "slot")
    in_specs = (P(seq, None), P("section", seq, None), P("section", seq))
    out_specs = (P("section", seq, None), P("section", seq, None, None))
    return jax.shard_map(
        per_device, mesh=split, in_specs=in_specs, out_specs=out_specs, check_vma=False
    )
```
